256 devices in a mesh: dp: 64 (over x, z, y_lo), mp: 4 (over y_hi, core).
Axes of the slice: x: 4, y: 4 (y_hi: 2, y_lo: 2; y = y_hi * 2 + y_lo), z: 8, core: 2. Of those that a mesh axis runs over, the one named last changes fastest.
Arguments:
- gate_pre: bfloat16 [16384, 12288], P('dp', 'mp'), may hold values from -6 to 6
- up_pre: bfloat16 [16384, 12288], P('dp', 'mp'), may hold values from -16 to 16
- out_grad: bfloat16 [16384, 3072], P('dp', 'mp'), may hold values from -0.046875 to 0.046875
Outputs:
- weight_grad: bfloat16 [12288, 3072], P(('mp', 'dp'))
The draws below stay inside these ranges and needn't reach their ends.
All inputs are finite; a program needn't handle non-finite values.
Results may differ from the reference program's by a relative error of at most 0.0049.
Values may be sent and summed in bfloat16 or wider, within the bound.
A program may use at most 128 MiB of HBM per device.

```python
import jax
import jax.numpy as jnp
from jax import lax

D = 3072
FF = 12288
TOK_DEV = 256
TOKENS = 16384
N_DP = 64


def with_spikes(result, key, source, target, blocks, factor):
    owner, partner = [(jnp.arange(result.shape[axis_at]) // (result.shape[axis_at] // blocks)).reshape([-1 if axis == axis_at else 1 for axis in range(result.ndim)]) for axis_at in (source, target)]
    chosen = jax.random.permutation(key, blocks)[partner]
    strong = (owner == chosen) | (owner == (partner + blocks // 2) % blocks)
    return jnp.where(strong, factor * result, result)


def shard_levels(rng, extent, shards, low, largest):
    def one(position, shards_of):
        draws = jax.random.uniform(jax.random.fold_in(jax.random.fold_in(rng, 6), position), (shards_of,), jnp.float32, low / len(shards), largest / len(shards))
        return jnp.repeat(jnp.exp(draws), extent[position] // shards_of).reshape((-1,) + (1,) * (len(extent) - position - 1))

    gain = one(*shards[0])
    for cut in shards[1:]:
        gain = gain * one(*cut)
    return gain


def gaussian(rng, dims, deviation, most, shards=(), dtype=jnp.bfloat16):
    factor_of = shard_levels(rng, dims, shards, -0.22, 0.18) if shards else 1.0
    entries = jax.random.normal(rng, dims, jnp.float32) * deviation * factor_of
    return jnp.minimum(jnp.maximum(entries, -most), most).astype(dtype)


def noise_with(key, extent, scale, most, shards, heavy, dtype=jnp.bfloat16):
    drawn = scale * jax.random.normal(key, extent, jnp.float32)
    if shards:
        drawn = drawn * shard_levels(key, extent, shards, -0.22, 0.18)
    return jnp.clip(with_spikes(drawn, jax.random.fold_in(key, 3), *heavy), -most, most).astype(dtype)


def setup_inputs(seed: int = 0) -> dict:
    key_list = jax.random.split(jax.random.key(seed), 4)
    return {
        "gate_pre": gaussian(key_list[0], (TOKENS, FF), 1.0, 6.0, ((0, 64), (1, 4))),
        "up_pre": noise_with(key_list[1], (TOKENS, FF), 1.0, 16.0, ((0, 64), (1, 4)), (0, 1, 64, 4.0)),
        "out_grad": gaussian(key_list[2], (TOKENS, D), TOKENS ** -0.5, 0.046875, ((0, 64), (1, 4))),
    }


def reference(gate_pre, up_pre, out_grad):
    gate_f = gate_pre.astype(jnp.float32)
    up_f = up_pre.astype(jnp.float32)
    hidden = (jax.nn.silu(gate_f) * up_f).astype(jnp.bfloat16)
    hidden_groups = hidden.reshape(N_DP, TOK_DEV, FF)
    grad_groups = out_grad.reshape(N_DP, TOK_DEV, D)

    def add_group(total, pair):
        hidden_part, grad_part = pair
        partial_value = jnp.dot(hidden_part.astype(jnp.float32).T, grad_part.astype(jnp.float32),
                          preferred_element_type=jnp.float32, precision=lax.Precision.HIGHEST)
        return total + partial_value, None

    total, _ = lax.scan(add_group, jnp.zeros((FF, D), jnp.float32), (hidden_groups, grad_groups))
    return total.astype(jnp.bfloat16)
```

```python
import functools

import jax
import jax.numpy as jnp
from jax import lax
from jax.experimental import pallas as pl
from jax.experimental.pallas import tpu as pltpu
from jax.sharding import PartitionSpec as P

MESH = pl.DeviceIdType.MESH
NX = 4
NZ = 8
OWN, LEFT, RIGHT, OPP = range(4)


def kernel(
    dims,
    gate_hbm,
    up_hbm,
    og_hbm,
    out_ref,
    gate,
    up,
    ht,
    hbuf,
    hrel,
    gbuf,
    zs,
    zr,
    fin,
    ys,
    yr,
    loc_sem,
    og_sem,
    gs_sem,
    gr_sem,
    gp_sem,
    cs_sem,
    cr_sem,
    hs_sem,
    hr_sem,
    zs_sem,
    zr_sem,
    ys_sem,
    yr_sem,
):
    tb, rows, w, nu, nz = dims
    far = nz // 2
    half_t = tb // 2
    dp, mp = lax.axis_index("dp"), lax.axis_index("mp")
    y = lax.rem(dp, 2)
    z = lax.rem(dp // 2, nz)
    x = dp // (2 * nz)
    core = lax.rem(mp, 2)
    half = mp // 2

    def at(xx, zz):
        return ((lax.rem(xx, NX) * nz + lax.rem(zz, nz)) * 2 + y, mp)

    right, left = at(x + 1, z), at(x + NX - 1, z)
    zright, zleft = at(x, z + 1), at(x, z + nz - 1)
    ypeer = (dp + 1 - 2 * y, mp)
    partner = (dp, mp + 1 - 2 * core)
    cross = (dp, mp + 2 - 4 * half)
    peers = (right, left, zright, zleft, ypeer, partner, cross)

    def unit(t, u, who):
        return (t * nu + u) * 2 + who

    def rcopy(src, dst, ssem, rsem, to):
        return pltpu.make_async_remote_copy(
            src_ref=src, dst_ref=dst, send_sem=ssem, recv_sem=rsem, device_id=to, device_id_type=MESH
        )

    ncol = gate.shape[0]
    wide = gate.shape[2]
    gate_copies = [
        pltpu.make_async_copy(gate_hbm.at[:, pl.ds(i * wide, wide)], gate.at[i], loc_sem.at[0, i]) for i in range(ncol)
    ]
    up_copies = [
        pltpu.make_async_copy(up_hbm.at[:, pl.ds(i * wide, wide)], up.at[i], loc_sem.at[1, i]) for i in range(ncol)
    ]
    og_copies = [
        pltpu.make_async_copy(og_hbm.at[:, pl.ds(u * w, w)], gbuf.at[unit(0, u, 0), OWN], og_sem.at[u])
        for u in range(nu)
    ]
    for c in og_copies + gate_copies + up_copies:
        c.start()

    barrier = pltpu.get_barrier_semaphore()
    for peer in peers:
        pl.semaphore_signal(barrier, inc=1, device_id=peer, device_id_type=MESH)
    pl.semaphore_wait(barrier, len(peers))

    FIRST, LAST = pl.ds(0, half_t), pl.ds(half_t, half_t)

    def g_own(t, u, i):
        k = t * nu + u
        src = gbuf.at[unit(t, u, 0), OWN]
        if i == 0:
            return rcopy(src, gbuf.at[unit(t, u, 0), LEFT], gs_sem.at[0, k], gr_sem.at[0, k], right)
        if i == 1:
            return rcopy(src, gbuf.at[unit(t, u, 0), RIGHT], gs_sem.at[1, k], gr_sem.at[1, k], left)
        return rcopy(src, gbuf.at[unit(t, u, 1), OWN], gs_sem.at[2, k], gp_sem.at[0, k], partner)

    def g_relay(t, u, i):
        k = t * nu + u
        own = unit(t, u, 0)
        if i == 0:
            return rcopy(
                gbuf.at[own, LEFT, FIRST], gbuf.at[own, OPP, FIRST], gs_sem.at[3, k], gr_sem.at[2, k], right
            )
        return rcopy(gbuf.at[own, RIGHT, LAST], gbuf.at[own, OPP, LAST], gs_sem.at[4, k], gr_sem.at[3, k], left)

    def g_give(t, u, i):
        k = t * nu + u
        own, his = unit(t, u, 0), unit(t, u, 1)
        if i < 2:
            slot = (LEFT, RIGHT)[i]
            return rcopy(gbuf.at[own, slot], gbuf.at[his, slot], gs_sem.at[5 + i, k], gp_sem.at[1 + i, k], partner)
        part = (FIRST, LAST)[i - 2]
        return rcopy(
            gbuf.at[own, OPP, part], gbuf.at[his, OPP, part], gs_sem.at[5 + i, k], gp_sem.at[1 + i, k], partner
        )

    def g_cross(u):
        return rcopy(
            gbuf.at[unit(0, u, 0), OWN], gbuf.at[unit(1, u, 0), OWN], cs_sem.at[u], cr_sem.at[u], cross
        )

    def send_own(t):
        def body(u, _):
            if t == 1:
                g_cross(u).wait_recv()
            for i in range(3):
                g_own(t, u, i).start()
            return 0

        lax.fori_loop(0, nu, body, 0)

    def relay(t):
        def body(u, _):
            g_own(t, u, 0).wait_recv()
            g_relay(t, u, 0).start()
            g_give(t, u, 0).start()
            g_own(t, u, 1).wait_recv()
            g_relay(t, u, 1).start()
            g_give(t, u, 1).start()
            return 0

        lax.fori_loop(0, nu, body, 0)

    def give_opp(t):
        def body(u, _):
            for i in range(2):
                g_relay(t, u, i).wait_recv()
                g_give(t, u, 2 + i).start()
            return 0

        lax.fori_loop(0, nu, body, 0)

    def z_of(o):
        odd = lax.rem(o, 2)
        rel = odd * (far - (o + 1) // 2) + (1 - odd) * (far + o // 2)
        return lax.rem(z + rel, nz)

    xr, xl, xo = lax.rem(x + 1, NX), lax.rem(x + NX - 1, NX), lax.rem(x + 2, NX)

    def h_copy(o, i):
        zi = z_of(o)
        if i == 0:
            pair, to = (ht.at[xr, zi], hbuf.at[0, zi]), right
        elif i == 1:
            pair, to = (ht.at[xl, zi], hbuf.at[1, zi]), left
        elif i == 2:
            pair, to = (ht.at[xo, zi, 0], hrel.at[0, zi]), right
        elif i == 3:
            pair, to = (ht.at[xo, zi, 1], hrel.at[1, zi]), left
        elif i == 4:
            pair, to = (hrel.at[0, zi], hbuf.at[2, zi, 0]), right
        else:
            pair, to = (hrel.at[1, zi], hbuf.at[2, zi, 1]), left
        return rcopy(pair[0], pair[1], hs_sem.at[i, o], hr_sem.at[i, o], to)

    def h_send(lo, hi):
        def body(o, _):
            for i in range(4):
                h_copy(o, i).start()
            return 0

        lax.fori_loop(lo, hi, body, 0)

    def h_relay(lo, hi):
        def body(o, _):
            for i in range(2):
                h_copy(o, 2 + i).wait_recv()
                h_copy(o, 4 + i).start()
            return 0

        lax.fori_loop(lo, hi, body, 0)

    def h_wait(lo, hi):
        def body(o, _):
            for i in (0, 1, 4, 5):
                h_copy(o, i).wait_recv()
            return 0

        lax.fori_loop(lo, hi, body, 0)

    def z_copy(direction, d, n):
        to = (zright, zleft)[direction]
        if d == far:
            src, dst = zs.at[direction, d - 1, n, direction], zr.at[direction, d - 1, n, direction]
        else:
            src, dst = zs.at[direction, d - 1, n], zr.at[direction, d - 1, n]
        return rcopy(src, dst, zs_sem.at[direction, d - 1, n], zr_sem.at[direction, d - 1, n], to)

    def y_copy(n):
        return rcopy(ys.at[n], yr.at[n], ys_sem.at[n], yr_sem.at[n], ypeer)

    def lhs(slot, zi):
        block = ht[x, zi] if slot == OWN else hbuf[slot - 1, zi]
        return block.reshape(2 * rows, tb)

    def product(n, zis):
        total = None
        for slot in range(4):
            left_side = [lhs(slot, zi) for zi in zis]
            block = left_side[0] if len(zis) == 1 else jnp.concatenate(left_side, axis=0)
            term = jnp.dot(block, gbuf[n, slot], preferred_element_type=jnp.float32)
            total = term if total is None else total + term
        return total.reshape(len(zis), 2, rows, w)

    def step(n, d):
        if d == far:
            p = product(n, [lax.rem(z + far, nz)])
            for direction in range(2):
                zs[direction, d - 1, n, direction] = p[0, direction].astype(jnp.bfloat16)
                z_copy(direction, d, n).start()
        elif d > 0:
            p = product(n, [lax.rem(z + d, nz), lax.rem(z + nz - d, nz)])
            for direction in range(2):
                z_copy(direction, d + 1, n).wait_recv()
                if d + 1 == far:
                    zs[direction, d - 1, n, direction] = (
                        p[direction, direction] + zr[direction, d, n, direction].astype(jnp.float32)
                    ).astype(jnp.bfloat16)
                    zs[direction, d - 1, n, 1 - direction] = p[direction, 1 - direction].astype(jnp.bfloat16)
                else:
                    zs[direction, d - 1, n] = (p[direction] + zr[direction, d, n].astype(jnp.float32)).astype(
                        jnp.bfloat16
                    )
                z_copy(direction, d, n).start()
        else:
            p = product(n, [z])[0]
            for direction in range(2):
                z_copy(direction, 1, n).wait_recv()
                p = p + zr[direction, 0, n].astype(jnp.float32)
            fin[n] = p
            ys[n] = fin[n, 1 - y].astype(jnp.bfloat16)
            y_copy(n).start()

    def phase(t, d):
        def body(u, _):
            step(unit(t, u, 0), d)
            if d == far:
                g_own(t, u, 2).wait_recv()
                for i in range(4):
                    g_give(t, u, i).wait_recv()
            step(unit(t, u, 1), d)
            return 0

        lax.fori_loop(0, nu, body, 0)

    def finish(t):
        def body(u, _):
            for who in range(2):
                n = unit(t, u, who)
                y_copy(n).wait_recv()
                q = (
                    (half + t - 2 * half * t) * 2 + (core + who - 2 * core * who)
                )
                column = pl.multiple_of((q * nu + u) * w, w)
                out_ref[:, pl.ds(column, w)] = (fin[n, y] + yr[n].astype(jnp.float32)).astype(jnp.bfloat16)
            return 0

        lax.fori_loop(0, nu, body, 0)

    for c in og_copies:
        c.wait()
    send_own(0)

    def cross_body(u, _):
        g_cross(u).start()
        return 0

    lax.fori_loop(0, nu, cross_body, 0)

    def silu_body(i, _):
        pltpu.make_async_copy(gate_hbm.at[:, pl.ds(pl.multiple_of(i * wide, 128), wide)], gate.at[i], loc_sem.at[0, i]).wait()
        pltpu.make_async_copy(up_hbm.at[:, pl.ds(pl.multiple_of(i * wide, 128), wide)], up.at[i], loc_sem.at[1, i]).wait()
        g = gate[i].astype(jnp.float32)
        h = (g / (1.0 + jnp.exp(-g)) * up[i].astype(jnp.float32)).astype(jnp.bfloat16)
        ht[i // (nz * 2 * rows // wide), pl.ds(lax.rem(i, nz * 2 * rows // wide) * (wide // (2 * rows)), wide // (2 * rows))] = (
            h.T.reshape(wide // (2 * rows), 2, rows, tb)
        )
        return 0

    lax.fori_loop(0, ncol, silu_body, 0)

    h_send(0, 3)
    relay(0)
    h_relay(0, 3)
    h_send(3, nz)
    give_opp(0)
    h_wait(0, 1)
    phase(0, far)
    h_wait(1, 3)
    phase(0, far - 1)
    h_relay(3, 5)
    for d in range(far - 2, 0, -1):
        o = 2 * (far - d) - 1
        h_wait(o, o + 2)
        phase(0, d)
        if d == 2:
            h_relay(5, nz)
            send_own(1)
    relay(1)
    h_wait(nz - 1, nz)
    phase(0, 0)
    give_opp(1)
    for d in range(far, -1, -1):
        phase(1, d)
        if d == far:
            finish(0)
    finish(1)

    def drain_g(u, _):
        for t in range(2):
            for i in range(3):
                g_own(t, u, i).wait_send()
            for i in range(2):
                g_relay(t, u, i).wait_send()
            for i in range(4):
                g_give(t, u, i).wait_send()
        g_cross(u).wait_send()
        return 0

    lax.fori_loop(0, nu, drain_g, 0)

    def drain_h(o, _):
        for i in range(6):
            h_copy(o, i).wait_send()
        return 0

    lax.fori_loop(0, nz, drain_h, 0)

    def drain_z(n, _):
        for d in range(1, far + 1):
            for direction in range(2):
                z_copy(direction, d, n).wait_send()
        y_copy(n).wait_send()
        return 0

    lax.fori_loop(0, 4 * nu, drain_z, 0)


def run(gate_pre, up_pre, out_grad, w=256, nz=NZ, interpret=False):
    tb, hidden = gate_pre.shape
    rows = hidden // (NX * nz * 2)
    nu = out_grad.shape[1] // w
    features = 4 * out_grad.shape[1]
    far = nz // 2
    bf16 = jnp.bfloat16
    wide = 2 * rows * nz // 2
    ncol = hidden // wide
    n = 4 * nu
    dma = pltpu.SemaphoreType.DMA
    return pl.pallas_call(
        functools.partial(kernel, (tb, rows, w, nu, nz)),
        out_shape=jax.ShapeDtypeStruct((rows, features), bf16),
        in_specs=[pl.BlockSpec(memory_space=pl.ANY)] * 3,
        out_specs=pl.BlockSpec(memory_space=pltpu.VMEM),
        scratch_shapes=[
            pltpu.VMEM((ncol, tb, wide), bf16),
            pltpu.VMEM((ncol, tb, wide), bf16),
            pltpu.VMEM((NX, nz, 2, rows, tb), bf16),
            pltpu.VMEM((3, nz, 2, rows, tb), bf16),
            pltpu.VMEM((2, nz, rows, tb), bf16),
            pltpu.VMEM((n, 4, tb, w), bf16),
            pltpu.VMEM((2, far, n, 2, rows, w), bf16),
            pltpu.VMEM((2, far, n, 2, rows, w), bf16),
            pltpu.VMEM((n, 2, rows, w), jnp.float32),
            pltpu.VMEM((n, rows, w), bf16),
            pltpu.VMEM((n, rows, w), bf16),
            dma((2, ncol)),
            dma((nu,)),
            dma((9, 2 * nu)),
            dma((4, 2 * nu)),
            dma((5, 2 * nu)),
            dma((nu,)),
            dma((nu,)),
            dma((6, nz)),
            dma((6, nz)),
            dma((2, far, n)),
            dma((2, far, n)),
            dma((n,)),
            dma((n,)),
        ],
        compiler_params=pltpu.CompilerParams(
            collective_id=0, has_side_effects=True, vmem_limit_bytes=60 * 1024 * 1024
        ),
        interpret=interpret,
    )(gate_pre, up_pre, out_grad)


def solution(mesh):
    return jax.shard_map(
        run,
        mesh=mesh,
        in_specs=(P("dp", "mp"), P("dp", "mp"), P("dp", "mp")),
        out_specs=P(("mp", "dp"), None),
        check_vma=False,
    )
```

```python
import functools

import jax
import jax.numpy as jnp
from jax import lax
from jax.experimental import pallas as pl
from jax.experimental.pallas import tpu as pltpu
from jax.sharding import PartitionSpec as P

MESH = pl.DeviceIdType.MESH
NX = 4
NZ = 8
OWN, LEFT, RIGHT, OPP = range(4)
Y_FIRST = ((1, 0), (1, 1))
ACROSS = (1, 2)


def kernel(
    dims,
    gate_hbm,
    up_hbm,
    og_hbm,
    out_ref,
    gate,
    up,
    ht,
    hbuf,
    hrel,
    gbuf,
    zs,
    zr,
    fin,
    ys,
    yr,
    loc_sem,
    og_sem,
    gs_sem,
    gr_sem,
    gp_sem,
    cs_sem,
    cr_sem,
    hs_sem,
    hr_sem,
    zs_sem,
    zr_sem,
    ys_sem,
    yr_sem,
    yps,
    ypr,
    yps_sem,
    ypr_sem,
    cxs_sem,
    cxr_sem,
):
    tb, rows, w, nu, nz = dims
    far = nz // 2
    half_t = tb // 2
    dp, mp = lax.axis_index("dp"), lax.axis_index("mp")
    y = lax.rem(dp, 2)
    z = lax.rem(dp // 2, nz)
    x = dp // (2 * nz)
    core = lax.rem(mp, 2)
    half = mp // 2

    def at(xx, zz):
        return ((lax.rem(xx, NX) * nz + lax.rem(zz, nz)) * 2 + y, mp)

    right, left = at(x + 1, z), at(x + NX - 1, z)
    zright, zleft = at(x, z + 1), at(x, z + nz - 1)
    ypeer = (dp + 1 - 2 * y, mp)
    partner = (dp, mp + 1 - 2 * core)
    cross = (dp, mp + 2 - 4 * half)
    peers = (right, left, zright, zleft, ypeer, partner, cross)

    def unit(t, u, who):
        return (t * nu + u) * 2 + who

    def rcopy(src, dst, ssem, rsem, to):
        return pltpu.make_async_remote_copy(
            src_ref=src, dst_ref=dst, send_sem=ssem, recv_sem=rsem, device_id=to, device_id_type=MESH
        )

    ncol = gate.shape[0]
    wide = gate.shape[2]
    gate_copies = [
        pltpu.make_async_copy(gate_hbm.at[:, pl.ds(i * wide, wide)], gate.at[i], loc_sem.at[0, i]) for i in range(ncol)
    ]
    up_copies = [
        pltpu.make_async_copy(up_hbm.at[:, pl.ds(i * wide, wide)], up.at[i], loc_sem.at[1, i]) for i in range(ncol)
    ]
    og_copies = [
        pltpu.make_async_copy(og_hbm.at[:, pl.ds(u * w, w)], gbuf.at[unit(0, u, 0), OWN], og_sem.at[u])
        for u in range(nu)
    ]
    for c in og_copies + gate_copies + up_copies:
        c.start()

    barrier = pltpu.get_barrier_semaphore()
    for peer in peers:
        pl.semaphore_signal(barrier, inc=1, device_id=peer, device_id_type=MESH)
    pl.semaphore_wait(barrier, len(peers))

    FIRST, LAST = pl.ds(0, half_t), pl.ds(half_t, half_t)

    def g_own(t, u, i):
        k = t * nu + u
        src = gbuf.at[unit(t, u, 0), OWN]
        if i == 0:
            return rcopy(src, gbuf.at[unit(t, u, 0), LEFT], gs_sem.at[0, k], gr_sem.at[0, k], right)
        if i == 1:
            return rcopy(src, gbuf.at[unit(t, u, 0), RIGHT], gs_sem.at[1, k], gr_sem.at[1, k], left)
        return rcopy(src, gbuf.at[unit(t, u, 1), OWN], gs_sem.at[2, k], gp_sem.at[0, k], partner)

    def g_relay(t, u, i):
        k = t * nu + u
        own = unit(t, u, 0)
        if i == 0:
            return rcopy(
                gbuf.at[own, LEFT, FIRST], gbuf.at[own, OPP, FIRST], gs_sem.at[3, k], gr_sem.at[2, k], right
            )
        return rcopy(gbuf.at[own, RIGHT, LAST], gbuf.at[own, OPP, LAST], gs_sem.at[4, k], gr_sem.at[3, k], left)

    def g_give(t, u, i):
        k = t * nu + u
        own, his = unit(t, u, 0), unit(t, u, 1)
        if i < 2:
            slot = (LEFT, RIGHT)[i]
            return rcopy(gbuf.at[own, slot], gbuf.at[his, slot], gs_sem.at[5 + i, k], gp_sem.at[1 + i, k], partner)
        part = (FIRST, LAST)[i - 2]
        return rcopy(
            gbuf.at[own, OPP, part], gbuf.at[his, OPP, part], gs_sem.at[5 + i, k], gp_sem.at[1 + i, k], partner
        )

    def g_cross(u):
        return rcopy(
            gbuf.at[unit(0, u, 0), OWN], gbuf.at[unit(1, u, 0), OWN], cs_sem.at[u], cr_sem.at[u], cross
        )

    def g_across(u, i):
        here, there = unit(0, u, 0), unit(1, u, 0)
        if i < 2:
            slot = (LEFT, RIGHT)[i]
            src, dst = gbuf.at[here, slot], gbuf.at[there, slot]
        else:
            part = (FIRST, LAST)[i - 2]
            src, dst = gbuf.at[here, OPP, part], gbuf.at[there, OPP, part]
        return rcopy(src, dst, cxs_sem.at[i, u], cxr_sem.at[i, u], cross)

    def across(t, u):
        return t == 1 and u in ACROSS

    def send_own(t, u):
        if t == 1:
            g_cross(u).wait_recv()
        for i in (2,) if across(t, u) else (0, 1, 2):
            g_own(t, u, i).start()

    def relay(t, u):
        for i in range(2):
            if across(t, u):
                g_across(u, i).wait_recv()
            else:
                g_own(t, u, i).wait_recv()
                g_relay(t, u, i).start()
            g_give(t, u, i).start()
            if across(1 - t, u):
                g_across(u, i).start()

    def give_opp(t, u):
        for i in range(2):
            if across(t, u):
                g_across(u, 2 + i).wait_recv()
            else:
                g_relay(t, u, i).wait_recv()
            g_give(t, u, 2 + i).start()
            if across(1 - t, u):
                g_across(u, 2 + i).start()

    def z_of(o):
        odd = lax.rem(o, 2)
        rel = odd * (far - (o + 1) // 2) + (1 - odd) * (far + o // 2)
        return lax.rem(z + rel, nz)

    xr, xl, xo = lax.rem(x + 1, NX), lax.rem(x + NX - 1, NX), lax.rem(x + 2, NX)

    def h_copy(o, i):
        zi = z_of(o)
        if i == 0:
            pair, to = (ht.at[xr, zi], hbuf.at[0, zi]), right
        elif i == 1:
            pair, to = (ht.at[xl, zi], hbuf.at[1, zi]), left
        elif i == 2:
            pair, to = (ht.at[xo, zi, 0], hrel.at[0, zi]), right
        elif i == 3:
            pair, to = (ht.at[xo, zi, 1], hrel.at[1, zi]), left
        elif i == 4:
            pair, to = (hrel.at[0, zi], hbuf.at[2, zi, 0]), right
        else:
            pair, to = (hrel.at[1, zi], hbuf.at[2, zi, 1]), left
        return rcopy(pair[0], pair[1], hs_sem.at[i, o], hr_sem.at[i, o], to)

    def h_send(lo, hi, kinds):
        def body(o, _):
            for i in kinds:
                h_copy(o, i).start()
            return 0

        lax.fori_loop(lo, hi, body, 0)

    def h_relay(lo, hi):
        def body(o, _):
            for i in range(2):
                h_copy(o, 2 + i).wait_recv()
                h_copy(o, 4 + i).start()
            return 0

        lax.fori_loop(lo, hi, body, 0)

    def h_wait(lo, hi):
        def body(o, _):
            for i in (0, 1, 4, 5):
                h_copy(o, i).wait_recv()
            return 0

        lax.fori_loop(lo, hi, body, 0)

    def z_copy(direction, d, n):
        to = (zright, zleft)[direction]
        if d == far:
            src, dst = zs.at[direction, d - 1, n, direction], zr.at[direction, d - 1, n, direction]
        else:
            src, dst = zs.at[direction, d - 1, n], zr.at[direction, d - 1, n]
        return rcopy(src, dst, zs_sem.at[direction, d - 1, n], zr_sem.at[direction, d - 1, n], to)

    def y_copy(n):
        return rcopy(ys.at[n], yr.at[n], ys_sem.at[n], yr_sem.at[n], ypeer)

    def lhs(slot, zi, yi):
        at_z = ht.at[x, zi] if slot == OWN else hbuf.at[slot - 1, zi]
        return at_z[...].reshape(2 * rows, tb) if yi is None else at_z[yi]

    def product(n, zis, yi=None):
        total = None
        for slot in range(4):
            left_side = [lhs(slot, zi, yi) for zi in zis]
            block = left_side[0] if len(zis) == 1 else jnp.concatenate(left_side, axis=0)
            term = jnp.dot(block, gbuf[n, slot], preferred_element_type=jnp.float32)
            total = term if total is None else total + term
        if yi is None:
            return total.reshape(len(zis), 2, rows, w)
        return total.reshape(len(zis), rows, w)

    def owners(d):
        if d == far:
            return [lax.rem(z + far, nz)]
        return [z] if d == 0 else [lax.rem(z + d, nz), lax.rem(z + nz - d, nz)]

    def y_first(t, u):
        return (t, u) in Y_FIRST

    def yp_copy(k, d):
        part = pl.ds(0, 1 if d in (0, far) else 2)
        return rcopy(yps.at[k, d, part], ypr.at[k, d, part], yps_sem.at[k, d], ypr_sem.at[k, d], ypeer)

    def zy_copy(direction, d, n):
        to = (zright, zleft)[direction]
        return rcopy(
            zs.at[direction, d - 1, n, 0],
            zr.at[direction, d - 1, n, 0],
            zs_sem.at[direction, d - 1, n],
            zr_sem.at[direction, d - 1, n],
            to,
        )

    def column(t, u, who):
        q = (half + t - 2 * half * t) * 2 + (core + who - 2 * core * who)
        return pl.ds(pl.multiple_of((q * nu + u) * w, w), w)

    def pre_step(t, u, who, d):
        n, k = unit(t, u, who), Y_FIRST.index((t, u)) * 2 + who
        p = product(n, owners(d), 1 - y).astype(jnp.bfloat16)
        for j in range(p.shape[0]):
            yps[k, d, j] = p[j]
        yp_copy(k, d).start()

    def step_y(t, u, who, d):
        n, k = unit(t, u, who), Y_FIRST.index((t, u)) * 2 + who
        p = product(n, owners(d), y)
        yp_copy(k, d).wait_recv()
        parts = [p[j] + ypr[k, d, j].astype(jnp.float32) for j in range(p.shape[0])]
        if d == 0:
            for direction in range(2):
                zy_copy(direction, 1, n).wait_recv()
                parts[0] = parts[0] + zr[direction, 0, n, 0].astype(jnp.float32)
            out_ref[:, column(t, u, who)] = parts[0].astype(jnp.bfloat16)
            return
        for direction in (who,) if d == far else (0, 1):
            part = parts[0 if d == far else direction]
            if d + 1 < far or (d + 1 == far and direction == who):
                zy_copy(direction, d + 1, n).wait_recv()
                part = part + zr[direction, d, n, 0].astype(jnp.float32)
            zs[direction, d - 1, n, 0] = part.astype(jnp.bfloat16)
            zy_copy(direction, d, n).start()

    def step(n, d):
        if d == far:
            p = product(n, [lax.rem(z + far, nz)])
            for direction in range(2):
                zs[direction, d - 1, n, direction] = p[0, direction].astype(jnp.bfloat16)
                z_copy(direction, d, n).start()
        elif d > 0:
            p = product(n, [lax.rem(z + d, nz), lax.rem(z + nz - d, nz)])
            for direction in range(2):
                z_copy(direction, d + 1, n).wait_recv()
                if d + 1 == far:
                    zs[direction, d - 1, n, direction] = (
                        p[direction, direction] + zr[direction, d, n, direction].astype(jnp.float32)
                    ).astype(jnp.bfloat16)
                    zs[direction, d - 1, n, 1 - direction] = p[direction, 1 - direction].astype(jnp.bfloat16)
                else:
                    zs[direction, d - 1, n] = (p[direction] + zr[direction, d, n].astype(jnp.float32)).astype(
                        jnp.bfloat16
                    )
                z_copy(direction, d, n).start()
        else:
            p = product(n, [z])[0]
            for direction in range(2):
                z_copy(direction, 1, n).wait_recv()
                p = p + zr[direction, 0, n].astype(jnp.float32)
            fin[n] = p
            ys[n] = fin[n, 1 - y].astype(jnp.bfloat16)
            y_copy(n).start()

    def arrived(t, u):
        g_own(t, u, 2).wait_recv()
        for i in range(4):
            g_give(t, u, i).wait_recv()

    def pre(t, u, d):
        if y_first(t, u):
            pre_step(t, u, 0, d)
            if d == far:
                arrived(t, u)
            pre_step(t, u, 1, d)

    def pair(t, u, d):
        if y_first(t, u):
            step_y(t, u, 0, d)
            step_y(t, u, 1, d)
            return
        step(unit(t, u, 0), d)
        if d == far:
            arrived(t, u)
        step(unit(t, u, 1), d)

    def finish(t):
        for u in range(nu):
            for who in range(2):
                if not y_first(t, u):
                    n = unit(t, u, who)
                    y_copy(n).wait_recv()
                    out_ref[:, column(t, u, who)] = (fin[n, y] + yr[n].astype(jnp.float32)).astype(jnp.bfloat16)

    og_copies[0].wait()
    send_own(0, 0)
    for c in og_copies[1:]:
        c.wait()

    def cross_body(u, _):
        g_cross(u).start()
        return 0

    lax.fori_loop(0, nu, cross_body, 0)

    def silu_body(i, _):
        pltpu.make_async_copy(gate_hbm.at[:, pl.ds(pl.multiple_of(i * wide, 128), wide)], gate.at[i], loc_sem.at[0, i]).wait()
        pltpu.make_async_copy(up_hbm.at[:, pl.ds(pl.multiple_of(i * wide, 128), wide)], up.at[i], loc_sem.at[1, i]).wait()
        g = gate[i].astype(jnp.float32)
        h = (g / (1.0 + jnp.exp(-g)) * up[i].astype(jnp.float32)).astype(jnp.bfloat16)
        ht[i // (nz * 2 * rows // wide), pl.ds(lax.rem(i, nz * 2 * rows // wide) * (wide // (2 * rows)), wide // (2 * rows))] = (
            h.T.reshape(wide // (2 * rows), 2, rows, tb)
        )
        return 0

    lax.fori_loop(0, ncol, silu_body, 0)

    h_send(0, 1, (2, 3))
    h_send(0, 1, (0, 1))
    send_own(0, 1)
    send_own(0, 2)
    relay(0, 0)
    h_relay(0, 1)
    relay(0, 1)
    send_own(1, 1)
    h_send(1, 4, (2, 3))
    relay(0, 2)
    give_opp(0, 0)
    h_send(4, 5, (2, 3))
    h_send(1, 2, (0, 1))
    h_wait(0, 1)
    pair(0, 0, 4)
    h_send(2, 3, (0, 1))
    give_opp(0, 1)
    h_relay(1, 4)
    pair(0, 1, 4)
    h_send(3, 4, (0, 1))
    give_opp(0, 2)
    h_relay(4, 5)
    relay(1, 1)
    h_send(4, 5, (0, 1))
    pair(0, 2, 4)
    send_own(1, 2)
    h_send(5, 7, (2, 3))
    h_send(5, 6, (0, 1))
    h_wait(1, 3)
    pair(0, 0, 3)
    h_send(6, 7, (0, 1))
    pair(0, 1, 3)
    send_own(1, 0)
    relay(1, 2)
    pair(0, 2, 3)
    h_relay(5, 7)
    give_opp(1, 1)
    h_send(7, 8, (2, 3))
    h_wait(3, 5)
    pair(0, 0, 2)
    h_send(7, 8, (0, 1))
    pre(1, 1, 4)
    pre(1, 1, 3)
    pre(1, 1, 2)
    give_opp(1, 2)
    pair(0, 1, 2)
    relay(1, 0)
    pair(1, 2, 4)
    pair(0, 2, 2)
    h_relay(7, 8)
    h_wait(5, 7)
    pre(1, 1, 1)
    pair(1, 1, 4)
    pair(0, 0, 1)
    give_opp(1, 0)
    pair(0, 1, 1)
    h_wait(7, 8)
    pre(1, 1, 0)
    pre(1, 0, 4)
    pre(1, 0, 3)
    pre(1, 0, 2)
    pair(1, 2, 3)
    pre(1, 0, 1)
    pair(1, 1, 3)
    pair(0, 2, 1)
    pre(1, 0, 0)
    pair(0, 0, 0)
    pair(1, 0, 4)
    pair(0, 1, 0)
    pair(1, 2, 2)
    pair(1, 1, 2)
    pair(0, 2, 0)
    pair(1, 0, 3)
    pair(1, 2, 1)
    pair(1, 1, 1)
    pair(1, 0, 2)
    pair(1, 2, 0)
    pair(1, 1, 0)
    pair(1, 0, 1)
    pair(1, 0, 0)
    finish(0)
    finish(1)

    for u in range(nu):
        for t in range(2):
            for i in (2,) if across(t, u) else (0, 1, 2):
                g_own(t, u, i).wait_send()
            for i in range(0 if across(t, u) else 2):
                g_relay(t, u, i).wait_send()
            for i in range(4):
                g_give(t, u, i).wait_send()
            for i in range(4 if across(t, u) else 0):
                g_across(u, i).wait_send()
            for who in range(2):
                n = unit(t, u, who)
                if y_first(t, u):
                    k = Y_FIRST.index((t, u)) * 2 + who
                    for d in range(far + 1):
                        yp_copy(k, d).wait_send()
                    for d in range(1, far + 1):
                        for direction in (who,) if d == far else (0, 1):
                            zy_copy(direction, d, n).wait_send()
                else:
                    for d in range(1, far + 1):
                        for direction in range(2):
                            z_copy(direction, d, n).wait_send()
                    y_copy(n).wait_send()
        g_cross(u).wait_send()

    def drain_h(o, _):
        for i in range(6):
            h_copy(o, i).wait_send()
        return 0

    lax.fori_loop(0, nz, drain_h, 0)


def run(gate_pre, up_pre, out_grad, w=256, nz=NZ, interpret=False):
    tb, hidden = gate_pre.shape
    rows = hidden // (NX * nz * 2)
    nu = out_grad.shape[1] // w
    features = 4 * out_grad.shape[1]
    far = nz // 2
    bf16 = jnp.bfloat16
    wide = 2 * rows * nz // 2
    ncol = hidden // wide
    n = 4 * nu
    dma = pltpu.SemaphoreType.DMA
    return pl.pallas_call(
        functools.partial(kernel, (tb, rows, w, nu, nz)),
        out_shape=jax.ShapeDtypeStruct((rows, features), bf16),
        in_specs=[pl.BlockSpec(memory_space=pl.ANY)] * 3,
        out_specs=pl.BlockSpec(memory_space=pltpu.VMEM),
        scratch_shapes=[
            pltpu.VMEM((ncol, tb, wide), bf16),
            pltpu.VMEM((ncol, tb, wide), bf16),
            pltpu.VMEM((NX, nz, 2, rows, tb), bf16),
            pltpu.VMEM((3, nz, 2, rows, tb), bf16),
            pltpu.VMEM((2, nz, rows, tb), bf16),
            pltpu.VMEM((n, 4, tb, w), bf16),
            pltpu.VMEM((2, far, n, 2, rows, w), bf16),
            pltpu.VMEM((2, far, n, 2, rows, w), bf16),
            pltpu.VMEM((n, 2, rows, w), jnp.float32),
            pltpu.VMEM((n, rows, w), bf16),
            pltpu.VMEM((n, rows, w), bf16),
            dma((2, ncol)),
            dma((nu,)),
            dma((9, 2 * nu)),
            dma((4, 2 * nu)),
            dma((5, 2 * nu)),
            dma((nu,)),
            dma((nu,)),
            dma((6, nz)),
            dma((6, nz)),
            dma((2, far, n)),
            dma((2, far, n)),
            dma((n,)),
            dma((n,)),
            pltpu.VMEM((2 * len(Y_FIRST), far + 1, 2, rows, w), bf16),
            pltpu.VMEM((2 * len(Y_FIRST), far + 1, 2, rows, w), bf16),
            dma((2 * len(Y_FIRST), far + 1)),
            dma((2 * len(Y_FIRST), far + 1)),
            dma((4, nu)),
            dma((4, nu)),
        ],
        compiler_params=pltpu.CompilerParams(
            collective_id=0, has_side_effects=True, vmem_limit_bytes=60 * 1024 * 1024
        ),
        interpret=interpret,
    )(gate_pre, up_pre, out_grad)


def solution(mesh):
    return jax.shard_map(
        run,
        mesh=mesh,
        in_specs=(P("dp", "mp"), P("dp", "mp"), P("dp", "mp")),
        out_specs=P(("mp", "dp"), None),
        check_vma=False,
    )
```

```python
import functools

import jax
import jax.numpy as jnp
from jax import lax
from jax.experimental import pallas as pl
from jax.experimental.pallas import tpu as pltpu
from jax.sharding import PartitionSpec as P

MESH = pl.DeviceIdType.MESH
NX = 4
NZ = 8
OWN, LEFT, RIGHT, OPP = range(4)
Y_FIRST = ((1, 0), (1, 1))
ACROSS = (1, 2)


def kernel(
    dims,
    gate_hbm,
    up_hbm,
    og_hbm,
    out_ref,
    gu,
    ht,
    hbuf,
    hrel,
    gbuf,
    zs,
    zr,
    fin,
    ys,
    yr,
    yps,
    ypr,
    loc_sem,
    og_sem,
    send_sem,
    zsend_sem,
    gr_sem,
    go_sem,
    gp_sem,
    cr_sem,
    ca_sem,
    hi_sem,
    hr_sem,
    zr_sem,
    yr_sem,
    ypr_sem,
):
    tb, rows, w, nu, nz = dims
    far = nz // 2
    half_t = tb // 2
    dp, mp = lax.axis_index("dp"), lax.axis_index("mp")
    y = lax.rem(dp, 2)
    z = lax.rem(dp // 2, nz)
    x = dp // (2 * nz)
    core = lax.rem(mp, 2)
    half = mp // 2

    def at(xx, zz):
        return ((lax.rem(xx, NX) * nz + lax.rem(zz, nz)) * 2 + y, mp)

    right, left = at(x + 1, z), at(x + NX - 1, z)
    zright, zleft = at(x, z + 1), at(x, z + nz - 1)
    ypeer = (dp + 1 - 2 * y, mp)
    partner = (dp, mp + 1 - 2 * core)
    cross = (dp, mp + 2 - 4 * half)
    peers = (right, left, zright, zleft, ypeer, partner, cross)

    def unit(t, u, who):
        return (t * nu + u) * 2 + who

    def rcopy(src, dst, ssem, rsem, to):
        return pltpu.make_async_remote_copy(
            src_ref=src, dst_ref=dst, send_sem=ssem, recv_sem=rsem, device_id=to, device_id_type=MESH
        )

    ncol, _, _, wide = gu.shape
    gu_copies = []
    for i in range(ncol):
        for j, source in enumerate((gate_hbm, up_hbm)):
            part = source.at[:, pl.ds(i * wide, wide)]
            gu_copies.append(pltpu.make_async_copy(part, gu.at[i, j], loc_sem.at[i]))
    og_copies = [
        pltpu.make_async_copy(og_hbm.at[:, pl.ds(u * w, w)], gbuf.at[unit(0, u, 0), OWN], og_sem.at[u])
        for u in range(nu)
    ]
    for c in og_copies + gu_copies:
        c.start()

    barrier = pltpu.get_barrier_semaphore()
    for peer in peers:
        pl.semaphore_signal(barrier, inc=1, device_id=peer, device_id_type=MESH)
    pl.semaphore_wait(barrier, len(peers))

    def wait_in(ref, sem):
        rcopy(ref, ref, sem, sem, partner).wait_recv()

    def wait_out(ref, sem):
        rcopy(ref, ref, sem, sem, partner).wait_send()

    to_x, to_partner, to_cross, of_h, to_y, to_yp = (send_sem.at[i] for i in range(6))

    FIRST, LAST = pl.ds(0, half_t), pl.ds(half_t, half_t)

    def g_own(t, u, i):
        k = t * nu + u
        src = gbuf.at[unit(t, u, 0), OWN]
        if i == 0:
            return rcopy(src, gbuf.at[unit(t, u, 0), LEFT], to_x, gr_sem.at[k], right)
        if i == 1:
            return rcopy(src, gbuf.at[unit(t, u, 0), RIGHT], to_x, gr_sem.at[k], left)
        return rcopy(src, gbuf.at[unit(t, u, 1), OWN], to_partner, gp_sem.at[k], partner)

    def g_relay(t, u, i):
        k = t * nu + u
        own = unit(t, u, 0)
        if i == 0:
            return rcopy(
                gbuf.at[own, LEFT, FIRST], gbuf.at[own, OPP, FIRST], to_x, go_sem.at[k], right
            )
        return rcopy(gbuf.at[own, RIGHT, LAST], gbuf.at[own, OPP, LAST], to_x, go_sem.at[k], left)

    def g_give(t, u, i):
        k = t * nu + u
        own, his = unit(t, u, 0), unit(t, u, 1)
        if i < 2:
            slot = (LEFT, RIGHT)[i]
            return rcopy(gbuf.at[own, slot], gbuf.at[his, slot], to_partner, gp_sem.at[k], partner)
        part = (FIRST, LAST)[i - 2]
        return rcopy(
            gbuf.at[own, OPP, part], gbuf.at[his, OPP, part], to_partner, gp_sem.at[k], partner
        )

    def g_cross(u):
        return rcopy(
            gbuf.at[unit(0, u, 0), OWN], gbuf.at[unit(1, u, 0), OWN], to_cross, cr_sem.at[u], cross
        )

    def g_across(u, i):
        here, there = unit(0, u, 0), unit(1, u, 0)
        if i < 2:
            slot = (LEFT, RIGHT)[i]
            src, dst = gbuf.at[here, slot], gbuf.at[there, slot]
        else:
            part = (FIRST, LAST)[i - 2]
            src, dst = gbuf.at[here, OPP, part], gbuf.at[there, OPP, part]
        return rcopy(src, dst, to_cross, ca_sem.at[i // 2, u], cross)

    def across(t, u):
        return t == 1 and u in ACROSS

    def send_own(t, u):
        if t == 1:
            g_cross(u).wait_recv()
        for i in (2,) if across(t, u) else (0, 1, 2):
            g_own(t, u, i).start()

    def relay(t, u):
        own = gbuf.at[unit(t, u, 0)]
        wait_in(own.at[pl.ds(LEFT, 2)], ca_sem.at[0, u] if across(t, u) else gr_sem.at[t * nu + u])
        for i in range(2):
            if not across(t, u):
                g_relay(t, u, i).start()
            g_give(t, u, i).start()
            if across(1 - t, u):
                g_across(u, i).start()

    def give_opp(t, u):
        own = gbuf.at[unit(t, u, 0)]
        wait_in(own.at[OPP], ca_sem.at[1, u] if across(t, u) else go_sem.at[t * nu + u])
        for i in range(2):
            g_give(t, u, 2 + i).start()
            if across(1 - t, u):
                g_across(u, 2 + i).start()

    def z_of(o):
        odd = lax.rem(o, 2)
        rel = odd * (far - (o + 1) // 2) + (1 - odd) * (far + o // 2)
        return lax.rem(z + rel, nz)

    xr, xl, xo = lax.rem(x + 1, NX), lax.rem(x + NX - 1, NX), lax.rem(x + 2, NX)

    def h_copy(o, i):
        zi = z_of(o)
        if i == 0:
            pair, to = (ht.at[xr, zi], hbuf.at[0, zi]), right
        elif i == 1:
            pair, to = (ht.at[xl, zi], hbuf.at[1, zi]), left
        elif i == 2:
            pair, to = (ht.at[xo, zi, 0], hrel.at[0, zi]), right
        elif i == 3:
            pair, to = (ht.at[xo, zi, 1], hrel.at[1, zi]), left
        elif i == 4:
            pair, to = (hrel.at[0, zi], hbuf.at[2, zi, 0]), right
        else:
            pair, to = (hrel.at[1, zi], hbuf.at[2, zi, 1]), left
        return rcopy(pair[0], pair[1], of_h, (hi_sem if i in (2, 3) else hr_sem).at[o], to)

    def h_send(lo, hi, kinds):
        def body(o, _):
            for i in kinds:
                h_copy(o, i).start()
            return 0

        lax.fori_loop(lo, hi, body, 0)

    def h_relay(lo, hi):
        def body(o, _):
            wait_in(hrel.at[:, z_of(o)], hi_sem.at[o])
            for i in range(2):
                h_copy(o, 4 + i).start()
            return 0

        lax.fori_loop(lo, hi, body, 0)

    def h_wait(lo, hi):
        def body(o, _):
            wait_in(hbuf.at[:, z_of(o)], hr_sem.at[o])
            return 0

        lax.fori_loop(lo, hi, body, 0)

    def z_copy(direction, d, n):
        to = (zright, zleft)[direction]
        if d == far:
            src, dst = zs.at[direction, d - 1, n, direction], zr.at[direction, d - 1, n, direction]
        else:
            src, dst = zs.at[direction, d - 1, n], zr.at[direction, d - 1, n]
        return rcopy(src, dst, zsend_sem.at[0], zr_sem.at[d - 1, n // 2], to)

    def y_copy(n):
        return rcopy(ys.at[n], yr.at[n], to_y, yr_sem.at[n // 2], ypeer)

    def lhs(slot, zi, yi):
        at_z = ht.at[x, zi] if slot == OWN else hbuf.at[slot - 1, zi]
        return at_z[...].reshape(2 * rows, tb) if yi is None else at_z[yi]

    def product(n, zis, yi=None):
        total = None
        for slot in range(4):
            left_side = [lhs(slot, zi, yi) for zi in zis]
            block = left_side[0] if len(zis) == 1 else jnp.concatenate(left_side, axis=0)
            term = jnp.dot(block, gbuf[n, slot], preferred_element_type=jnp.float32)
            total = term if total is None else total + term
        if yi is None:
            return total.reshape(len(zis), 2, rows, w)
        return total.reshape(len(zis), rows, w)

    def owners(d):
        if d == far:
            return [lax.rem(z + far, nz)]
        return [z] if d == 0 else [lax.rem(z + d, nz), lax.rem(z + nz - d, nz)]

    def y_first(t, u):
        return (t, u) in Y_FIRST

    def yp_copy(k, d):
        part = pl.ds(0, 1 if d in (0, far) else 2)
        return rcopy(yps.at[k, d, part], ypr.at[k, d, part], to_yp, ypr_sem.at[k // 2, d], ypeer)

    def zy_copy(direction, d, n):
        to = (zright, zleft)[direction]
        return rcopy(
            zs.at[direction, d - 1, n, 0],
            zr.at[direction, d - 1, n, 0],
            zsend_sem.at[1],
            zr_sem.at[d - 1, n // 2],
            to,
        )

    def column(t, u, who):
        q = (half + t - 2 * half * t) * 2 + (core + who - 2 * core * who)
        return pl.ds(pl.multiple_of((q * nu + u) * w, w), w)

    def pre_step(t, u, who, d):
        n, k = unit(t, u, who), Y_FIRST.index((t, u)) * 2 + who
        p = product(n, owners(d), 1 - y).astype(jnp.bfloat16)
        for j in range(p.shape[0]):
            yps[k, d, j] = p[j]
        yp_copy(k, d).start()

    def step_y(t, u, who, d):
        n, k = unit(t, u, who), Y_FIRST.index((t, u)) * 2 + who
        p = product(n, owners(d), y)
        parts = [p[j] + ypr[k, d, j].astype(jnp.float32) for j in range(p.shape[0])]
        if d == 0:
            for direction in range(2):
                parts[0] = parts[0] + zr[direction, 0, n, 0].astype(jnp.float32)
            out_ref[:, column(t, u, who)] = parts[0].astype(jnp.bfloat16)
            return
        for direction in (who,) if d == far else (0, 1):
            part = parts[0 if d == far else direction]
            if d + 1 < far or (d + 1 == far and direction == who):
                part = part + zr[direction, d, n, 0].astype(jnp.float32)
            zs[direction, d - 1, n, 0] = part.astype(jnp.bfloat16)
            zy_copy(direction, d, n).start()

    def step(n, d):
        if d == far:
            p = product(n, [lax.rem(z + far, nz)])
            for direction in range(2):
                zs[direction, d - 1, n, direction] = p[0, direction].astype(jnp.bfloat16)
                z_copy(direction, d, n).start()
        elif d > 0:
            p = product(n, [lax.rem(z + d, nz), lax.rem(z + nz - d, nz)])
            for direction in range(2):
                if d + 1 == far:
                    zs[direction, d - 1, n, direction] = (
                        p[direction, direction] + zr[direction, d, n, direction].astype(jnp.float32)
                    ).astype(jnp.bfloat16)
                    zs[direction, d - 1, n, 1 - direction] = p[direction, 1 - direction].astype(jnp.bfloat16)
                else:
                    zs[direction, d - 1, n] = (p[direction] + zr[direction, d, n].astype(jnp.float32)).astype(
                        jnp.bfloat16
                    )
                z_copy(direction, d, n).start()
        else:
            p = product(n, [z])[0]
            for direction in range(2):
                p = p + zr[direction, 0, n].astype(jnp.float32)
            fin[n] = p
            ys[n] = fin[n, 1 - y].astype(jnp.bfloat16)
            y_copy(n).start()

    def arrived(t, u):
        wait_in(gbuf.at[unit(t, u, 1)], gp_sem.at[t * nu + u])

    def pre(t, u, d):
        if y_first(t, u):
            pre_step(t, u, 0, d)
            if d == far:
                arrived(t, u)
            pre_step(t, u, 1, d)

    def z_in(t, u, d):
        both = pl.ds(unit(t, u, 0), 2)
        if y_first(t, u):
            ref = zr.at[0, far - 1, both, 0] if d == far else zr.at[:, d - 1, both, 0]
        else:
            ref = zr.at[0, far - 1, both] if d == far else zr.at[:, d - 1, both]
        wait_in(ref, zr_sem.at[d - 1, unit(t, u, 0) // 2])

    def pair(t, u, d):
        if d < far:
            z_in(t, u, d + 1)
        if y_first(t, u):
            k = Y_FIRST.index((t, u))
            wait_in(ypr.at[pl.ds(2 * k, 2), d, pl.ds(0, 1 if d in (0, far) else 2)], ypr_sem.at[k, d])
            step_y(t, u, 0, d)
            step_y(t, u, 1, d)
            return
        step(unit(t, u, 0), d)
        if d == far:
            arrived(t, u)
        step(unit(t, u, 1), d)

    def finish(t):
        for u in range(nu):
            if y_first(t, u):
                continue
            wait_in(yr.at[pl.ds(unit(t, u, 0), 2)], yr_sem.at[t * nu + u])
            for who in range(2):
                n = unit(t, u, who)
                out_ref[:, column(t, u, who)] = (fin[n, y] + yr[n].astype(jnp.float32)).astype(jnp.bfloat16)

    og_copies[0].wait()
    send_own(0, 0)
    for c in og_copies[1:]:
        c.wait()

    def cross_body(u, _):
        g_cross(u).start()
        return 0

    lax.fori_loop(0, nu, cross_body, 0)

    def silu_body(i, _):
        pltpu.make_async_copy(gu.at[i], gu.at[i], loc_sem.at[i]).wait()
        g = gu[i, 0].astype(jnp.float32)
        h = (g / (1.0 + jnp.exp(-g)) * gu[i, 1].astype(jnp.float32)).astype(jnp.bfloat16)
        ht[i // (nz * 2 * rows // wide), pl.ds(lax.rem(i, nz * 2 * rows // wide) * (wide // (2 * rows)), wide // (2 * rows))] = (
            h.T.reshape(wide // (2 * rows), 2, rows, tb)
        )
        return 0

    lax.fori_loop(0, ncol, silu_body, 0)

    h_send(0, 1, (2, 3))
    h_send(0, 1, (0, 1))
    send_own(0, 1)
    send_own(0, 2)
    relay(0, 0)
    h_relay(0, 1)
    relay(0, 1)
    send_own(1, 1)
    h_send(1, 4, (2, 3))
    relay(0, 2)
    give_opp(0, 0)
    h_send(4, 5, (2, 3))
    h_send(1, 2, (0, 1))
    h_wait(0, 1)
    pair(0, 0, 4)
    h_send(2, 3, (0, 1))
    give_opp(0, 1)
    h_relay(1, 4)
    pair(0, 1, 4)
    h_send(3, 4, (0, 1))
    give_opp(0, 2)
    h_relay(4, 5)
    relay(1, 1)
    h_send(4, 5, (0, 1))
    pair(0, 2, 4)
    send_own(1, 2)
    h_send(5, 7, (2, 3))
    h_send(5, 6, (0, 1))
    h_wait(1, 3)
    pair(0, 0, 3)
    h_send(6, 7, (0, 1))
    pair(0, 1, 3)
    send_own(1, 0)
    relay(1, 2)
    pair(0, 2, 3)
    h_relay(5, 7)
    give_opp(1, 1)
    h_send(7, 8, (2, 3))
    h_wait(3, 5)
    pair(0, 0, 2)
    h_send(7, 8, (0, 1))
    pre(1, 1, 4)
    pre(1, 1, 3)
    pre(1, 1, 2)
    give_opp(1, 2)
    pair(0, 1, 2)
    relay(1, 0)
    pair(1, 2, 4)
    pair(0, 2, 2)
    h_relay(7, 8)
    h_wait(5, 7)
    pre(1, 1, 1)
    pair(1, 1, 4)
    pair(0, 0, 1)
    give_opp(1, 0)
    pair(0, 1, 1)
    h_wait(7, 8)
    pre(1, 1, 0)
    pre(1, 0, 4)
    pre(1, 0, 3)
    pre(1, 0, 2)
    pair(1, 2, 3)
    pre(1, 0, 1)
    pair(1, 1, 3)
    pair(0, 2, 1)
    pre(1, 0, 0)
    pair(0, 0, 0)
    pair(1, 0, 4)
    pair(0, 1, 0)
    pair(1, 2, 2)
    pair(1, 1, 2)
    pair(0, 2, 0)
    pair(1, 0, 3)
    pair(1, 2, 1)
    pair(1, 1, 1)
    pair(1, 0, 2)
    pair(1, 2, 0)
    pair(1, 1, 0)
    pair(1, 0, 1)
    pair(1, 0, 0)
    finish(0)
    finish(1)

    n_x, n_c, n_p = 2 * nu - len(ACROSS), 1 + len(ACROSS), len(Y_FIRST)
    wait_out(gbuf.at[pl.ds(0, n_x), pl.ds(0, 3)], to_x)
    wait_out(gbuf.at[pl.ds(0, 2 * nu)], to_partner)
    wait_out(gbuf.at[pl.ds(0, n_c), pl.ds(0, 3)], to_cross)
    wait_out(ht, of_h)
    wait_out(zs.at[:, pl.ds(0, 2 * nu - n_p), pl.ds(0, 2 * far - 1)], zsend_sem.at[0])
    wait_out(zs.at[0, pl.ds(0, n_p), pl.ds(0, 2 * far - 1)], zsend_sem.at[1])
    wait_out(ys.at[pl.ds(0, 4 * nu - 2 * n_p)], to_y)
    wait_out(yps.at[:, pl.ds(0, far)], to_yp)


def run(gate_pre, up_pre, out_grad, w=256, nz=NZ, interpret=False):
    tb, hidden = gate_pre.shape
    rows = hidden // (NX * nz * 2)
    nu = out_grad.shape[1] // w
    features = 4 * out_grad.shape[1]
    far = nz // 2
    bf16 = jnp.bfloat16
    wide = 2 * rows * nz // 2
    ncol = hidden // wide
    n = 4 * nu
    dma = pltpu.SemaphoreType.DMA
    return pl.pallas_call(
        functools.partial(kernel, (tb, rows, w, nu, nz)),
        out_shape=jax.ShapeDtypeStruct((rows, features), bf16),
        in_specs=[pl.BlockSpec(memory_space=pl.ANY)] * 3,
        out_specs=pl.BlockSpec(memory_space=pltpu.VMEM),
        scratch_shapes=[
            pltpu.VMEM((ncol, 2, tb, wide), bf16),
            pltpu.VMEM((NX, nz, 2, rows, tb), bf16),
            pltpu.VMEM((3, nz, 2, rows, tb), bf16),
            pltpu.VMEM((2, nz, rows, tb), bf16),
            pltpu.VMEM((n, 4, tb, w), bf16),
            pltpu.VMEM((2, far, n, 2, rows, w), bf16),
            pltpu.VMEM((2, far, n, 2, rows, w), bf16),
            pltpu.VMEM((n, 2, rows, w), jnp.float32),
            pltpu.VMEM((n, rows, w), bf16),
            pltpu.VMEM((n, rows, w), bf16),
            pltpu.VMEM((2 * len(Y_FIRST), far + 1, 2, rows, w), bf16),
            pltpu.VMEM((2 * len(Y_FIRST), far + 1, 2, rows, w), bf16),
            dma((ncol,)),
            dma((nu,)),
            dma((6,)),
            dma((2,)),
            dma((2 * nu,)),
            dma((2 * nu,)),
            dma((2 * nu,)),
            dma((nu,)),
            dma((2, nu)),
            dma((nz,)),
            dma((nz,)),
            dma((far, 2 * nu)),
            dma((2 * nu,)),
            dma((len(Y_FIRST), far + 1)),
        ],
        compiler_params=pltpu.CompilerParams(
            collective_id=0, has_side_effects=True, vmem_limit_bytes=60 * 1024 * 1024
        ),
        interpret=interpret,
    )(gate_pre, up_pre, out_grad)


def solution(mesh):
    return jax.shard_map(
        run,
        mesh=mesh,
        in_specs=(P("dp", "mp"), P("dp", "mp"), P("dp", "mp")),
        out_specs=P(("mp", "dp"), None),
        check_vma=False,
    )
```

```python
import functools

import jax
import jax.numpy as jnp
from jax import lax
from jax.experimental import pallas as pl
from jax.experimental.pallas import tpu as pltpu
from jax.sharding import PartitionSpec as P

MESH = pl.DeviceIdType.MESH
NX = 4
NZ = 8
OWN, LEFT, RIGHT, OPP = range(4)
Y_FIRST = ((1, 0), (1, 1))
ACROSS = (1, 2)


def kernel(
    dims,
    gate_hbm,
    up_hbm,
    og_hbm,
    out_ref,
    gu,
    ht,
    hbuf,
    hrel,
    gbuf,
    zs,
    zr,
    fin,
    ys,
    yr,
    yps,
    ypr,
    loc_sem,
    og_sem,
    send_sem,
    zsend_sem,
    gr_sem,
    go_sem,
    gp_sem,
    cr_sem,
    ca_sem,
    hi_sem,
    hr_sem,
    zr_sem,
    yr_sem,
    ypr_sem,
):
    tb, rows, w, nu, nz = dims
    far = nz // 2
    half_t = tb // 2
    dp, mp = lax.axis_index("dp"), lax.axis_index("mp")
    y = lax.rem(dp, 2)
    z = lax.rem(dp // 2, nz)
    x = dp // (2 * nz)
    core = lax.rem(mp, 2)
    half = mp // 2

    def at(xx, zz):
        return ((lax.rem(xx, NX) * nz + lax.rem(zz, nz)) * 2 + y, mp)

    right, left = at(x + 1, z), at(x + NX - 1, z)
    zright, zleft = at(x, z + 1), at(x, z + nz - 1)
    ypeer = (dp + 1 - 2 * y, mp)
    partner = (dp, mp + 1 - 2 * core)
    cross = (dp, mp + 2 - 4 * half)
    peers = (right, left, zright, zleft, ypeer, partner, cross)

    def unit(t, u, who):
        return (t * nu + u) * 2 + who

    def rcopy(src, dst, ssem, rsem, to):
        return pltpu.make_async_remote_copy(
            src_ref=src, dst_ref=dst, send_sem=ssem, recv_sem=rsem, device_id=to, device_id_type=MESH
        )

    ncol, _, _, wide = gu.shape
    gu_copies = []
    for i in range(ncol):
        for j, source in enumerate((gate_hbm, up_hbm)):
            part = source.at[:, pl.ds(i * wide, wide)]
            gu_copies.append(pltpu.make_async_copy(part, gu.at[i, j], loc_sem.at[i]))
    og_copies = [
        pltpu.make_async_copy(og_hbm.at[:, pl.ds(u * w, w)], gbuf.at[unit(0, u, 0), OWN], og_sem.at[u])
        for u in range(nu)
    ]
    for c in og_copies + gu_copies:
        c.start()

    barrier = pltpu.get_barrier_semaphore()
    for peer in peers:
        pl.semaphore_signal(barrier, inc=1, device_id=peer, device_id_type=MESH)
    pl.semaphore_wait(barrier, len(peers))

    def wait_in(ref, sem):
        rcopy(ref, ref, sem, sem, partner).wait_recv()

    def wait_out(ref, sem):
        rcopy(ref, ref, sem, sem, partner).wait_send()

    to_x, to_partner, to_cross, of_h, to_y, to_yp = (send_sem.at[i] for i in range(6))

    FIRST, LAST = pl.ds(0, half_t), pl.ds(half_t, half_t)

    def g_own(t, u, i):
        k = t * nu + u
        src = gbuf.at[unit(t, u, 0), OWN]
        if i == 0:
            return rcopy(src, gbuf.at[unit(t, u, 0), LEFT], to_x, gr_sem.at[k], right)
        if i == 1:
            return rcopy(src, gbuf.at[unit(t, u, 0), RIGHT], to_x, gr_sem.at[k], left)
        return rcopy(src, gbuf.at[unit(t, u, 1), OWN], to_partner, gp_sem.at[k], partner)

    def g_relay(t, u, i):
        k = t * nu + u
        own = unit(t, u, 0)
        if i == 0:
            return rcopy(
                gbuf.at[own, LEFT, FIRST], gbuf.at[own, OPP, FIRST], to_x, go_sem.at[k], right
            )
        return rcopy(gbuf.at[own, RIGHT, LAST], gbuf.at[own, OPP, LAST], to_x, go_sem.at[k], left)

    def g_give(t, u, i):
        k = t * nu + u
        own, his = unit(t, u, 0), unit(t, u, 1)
        if i < 2:
            slot = (LEFT, RIGHT)[i]
            return rcopy(gbuf.at[own, slot], gbuf.at[his, slot], to_partner, gp_sem.at[k], partner)
        part = (FIRST, LAST)[i - 2]
        return rcopy(
            gbuf.at[own, OPP, part], gbuf.at[his, OPP, part], to_partner, gp_sem.at[k], partner
        )

    def g_cross(u):
        return rcopy(
            gbuf.at[unit(0, u, 0), OWN], gbuf.at[unit(1, u, 0), OWN], to_cross, cr_sem.at[u], cross
        )

    def g_across(u, i):
        here, there = unit(0, u, 0), unit(1, u, 0)
        if i < 2:
            slot = (LEFT, RIGHT)[i]
            src, dst = gbuf.at[here, slot], gbuf.at[there, slot]
        else:
            part = (FIRST, LAST)[i - 2]
            src, dst = gbuf.at[here, OPP, part], gbuf.at[there, OPP, part]
        return rcopy(src, dst, to_cross, ca_sem.at[i // 2, u], cross)

    def across(t, u):
        return t == 1 and u in ACROSS

    def send_own(t, u):
        if t == 1:
            g_cross(u).wait_recv()
        for i in (2,) if across(t, u) else (0, 1, 2):
            g_own(t, u, i).start()

    def relay(t, u):
        own = gbuf.at[unit(t, u, 0)]
        wait_in(own.at[pl.ds(LEFT, 2)], ca_sem.at[0, u] if across(t, u) else gr_sem.at[t * nu + u])
        for i in range(2):
            if not across(t, u):
                g_relay(t, u, i).start()
            g_give(t, u, i).start()
            if across(1 - t, u):
                g_across(u, i).start()

    def give_opp(t, u):
        own = gbuf.at[unit(t, u, 0)]
        wait_in(own.at[OPP], ca_sem.at[1, u] if across(t, u) else go_sem.at[t * nu + u])
        for i in range(2):
            g_give(t, u, 2 + i).start()
            if across(1 - t, u):
                g_across(u, 2 + i).start()

    def z_of(o):
        odd = lax.rem(o, 2)
        rel = odd * (far - (o + 1) // 2) + (1 - odd) * (far + o // 2)
        return lax.rem(z + rel, nz)

    xr, xl, xo = lax.rem(x + 1, NX), lax.rem(x + NX - 1, NX), lax.rem(x + 2, NX)

    def h_copy(o, i):
        zi = z_of(o)
        if i == 0:
            pair, to = (ht.at[xr, zi], hbuf.at[0, zi]), right
        elif i == 1:
            pair, to = (ht.at[xl, zi], hbuf.at[1, zi]), left
        elif i == 2:
            pair, to = (ht.at[xo, zi, 0], hrel.at[0, zi]), right
        elif i == 3:
            pair, to = (ht.at[xo, zi, 1], hrel.at[1, zi]), left
        elif i == 4:
            pair, to = (hrel.at[0, zi], hbuf.at[2, zi, 0]), right
        else:
            pair, to = (hrel.at[1, zi], hbuf.at[2, zi, 1]), left
        return rcopy(pair[0], pair[1], of_h, (hi_sem if i in (2, 3) else hr_sem).at[o], to)

    def h_send(lo, hi, kinds):
        def body(o, _):
            for i in kinds:
                h_copy(o, i).start()
            return 0

        lax.fori_loop(lo, hi, body, 0)

    def h_relay(lo, hi):
        def body(o, _):
            wait_in(hrel.at[:, z_of(o)], hi_sem.at[o])
            for i in range(2):
                h_copy(o, 4 + i).start()
            return 0

        lax.fori_loop(lo, hi, body, 0)

    def h_wait(lo, hi):
        def body(o, _):
            wait_in(hbuf.at[:, z_of(o)], hr_sem.at[o])
            return 0

        lax.fori_loop(lo, hi, body, 0)

    def z_copy(direction, d, n):
        to = (zright, zleft)[direction]
        if d == far:
            src, dst = zs.at[direction, d - 1, n, direction], zr.at[direction, d - 1, n, direction]
        else:
            src, dst = zs.at[direction, d - 1, n], zr.at[direction, d - 1, n]
        return rcopy(src, dst, zsend_sem.at[0], zr_sem.at[d - 1, n], to)

    def y_copy(n):
        return rcopy(ys.at[n], yr.at[n], to_y, yr_sem.at[n // 2], ypeer)

    def lhs(slot, zi, yi):
        at_z = ht.at[x, zi] if slot == OWN else hbuf.at[slot - 1, zi]
        return at_z[...].reshape(2 * rows, tb) if yi is None else at_z[yi]

    def product(n, zis, yi=None):
        total = None
        for slot in range(4):
            left_side = [lhs(slot, zi, yi) for zi in zis]
            block = left_side[0] if len(zis) == 1 else jnp.concatenate(left_side, axis=0)
            term = jnp.dot(block, gbuf[n, slot], preferred_element_type=jnp.float32)
            total = term if total is None else total + term
        if yi is None:
            return total.reshape(len(zis), 2, rows, w)
        return total.reshape(len(zis), rows, w)

    def owners(d):
        if d == far:
            return [lax.rem(z + far, nz)]
        return [z] if d == 0 else [lax.rem(z + d, nz), lax.rem(z + nz - d, nz)]

    def y_first(t, u):
        return (t, u) in Y_FIRST

    def yp_copy(k, d):
        part = pl.ds(0, 1 if d in (0, far) else 2)
        return rcopy(yps.at[k, d, part], ypr.at[k, d, part], to_yp, ypr_sem.at[k, d], ypeer)

    def zy_copy(direction, d, n):
        to = (zright, zleft)[direction]
        return rcopy(
            zs.at[direction, d - 1, n, 0],
            zr.at[direction, d - 1, n, 0],
            zsend_sem.at[1],
            zr_sem.at[d - 1, n],
            to,
        )

    def column(t, u, who):
        q = (half + t - 2 * half * t) * 2 + (core + who - 2 * core * who)
        return pl.ds(pl.multiple_of((q * nu + u) * w, w), w)

    def pre_step(t, u, who, ds):
        n, k = unit(t, u, who), Y_FIRST.index((t, u)) * 2 + who
        p = product(n, [zi for d in ds for zi in owners(d)], 1 - y).astype(jnp.bfloat16)
        first = 0
        for d in ds:
            count = len(owners(d))
            for j in range(count):
                yps[k, d, j] = p[first + j]
            yp_copy(k, d).start()
            first += count

    def step_y(t, u, who, d):
        n, k = unit(t, u, who), Y_FIRST.index((t, u)) * 2 + who
        p = product(n, owners(d), y)
        part = pl.ds(0, 1 if d in (0, far) else 2)
        wait_in(ypr.at[k, d, part], ypr_sem.at[k, d])
        if d < far:
            wait_in(zr.at[who, d, n, 0] if d + 1 == far else zr.at[:, d, n, 0], zr_sem.at[d, n])
        parts = [p[j] + ypr[k, d, j].astype(jnp.float32) for j in range(p.shape[0])]
        if d == 0:
            for direction in range(2):
                parts[0] = parts[0] + zr[direction, 0, n, 0].astype(jnp.float32)
            out_ref[:, column(t, u, who)] = parts[0].astype(jnp.bfloat16)
            return
        for direction in (who,) if d == far else (0, 1):
            part = parts[0 if d == far else direction]
            if d + 1 < far or (d + 1 == far and direction == who):
                part = part + zr[direction, d, n, 0].astype(jnp.float32)
            zs[direction, d - 1, n, 0] = part.astype(jnp.bfloat16)
            zy_copy(direction, d, n).start()

    def step(n, d):
        if d == far:
            p = product(n, [lax.rem(z + far, nz)])
            for direction in range(2):
                zs[direction, d - 1, n, direction] = p[0, direction].astype(jnp.bfloat16)
                z_copy(direction, d, n).start()
        elif d > 0:
            p = product(n, [lax.rem(z + d, nz), lax.rem(z + nz - d, nz)])
            wait_in(zr.at[0, d, n] if d + 1 == far else zr.at[:, d, n], zr_sem.at[d, n])
            for direction in range(2):
                if d + 1 == far:
                    zs[direction, d - 1, n, direction] = (
                        p[direction, direction] + zr[direction, d, n, direction].astype(jnp.float32)
                    ).astype(jnp.bfloat16)
                    zs[direction, d - 1, n, 1 - direction] = p[direction, 1 - direction].astype(jnp.bfloat16)
                else:
                    zs[direction, d - 1, n] = (p[direction] + zr[direction, d, n].astype(jnp.float32)).astype(
                        jnp.bfloat16
                    )
                z_copy(direction, d, n).start()
        else:
            p = product(n, [z])[0]
            wait_in(zr.at[:, 0, n], zr_sem.at[0, n])
            for direction in range(2):
                p = p + zr[direction, 0, n].astype(jnp.float32)
            fin[n] = p
            ys[n] = fin[n, 1 - y].astype(jnp.bfloat16)
            y_copy(n).start()

    def arrived(t, u):
        wait_in(gbuf.at[unit(t, u, 1)], gp_sem.at[t * nu + u])

    def pre(t, u, *ds):
        pre_step(t, u, 0, ds)
        if far in ds:
            arrived(t, u)
        pre_step(t, u, 1, ds)

    def pair(t, u, d):
        if y_first(t, u):
            step_y(t, u, 0, d)
            step_y(t, u, 1, d)
            return
        step(unit(t, u, 0), d)
        if d == far:
            arrived(t, u)
        step(unit(t, u, 1), d)

    def finish(t):
        for u in range(nu):
            if y_first(t, u):
                continue
            wait_in(yr.at[pl.ds(unit(t, u, 0), 2)], yr_sem.at[t * nu + u])
            for who in range(2):
                n = unit(t, u, who)
                out_ref[:, column(t, u, who)] = (fin[n, y] + yr[n].astype(jnp.float32)).astype(jnp.bfloat16)

    og_copies[0].wait()
    send_own(0, 0)
    for c in og_copies[1:]:
        c.wait()

    def cross_body(u, _):
        g_cross(u).start()
        return 0

    lax.fori_loop(0, nu, cross_body, 0)

    def silu_body(i, _):
        pltpu.make_async_copy(gu.at[i], gu.at[i], loc_sem.at[i]).wait()
        g = gu[i, 0].astype(jnp.float32)
        h = (g / (1.0 + jnp.exp(-g)) * gu[i, 1].astype(jnp.float32)).astype(jnp.bfloat16)
        ht[i // (nz * 2 * rows // wide), pl.ds(lax.rem(i, nz * 2 * rows // wide) * (wide // (2 * rows)), wide // (2 * rows))] = (
            h.T.reshape(wide // (2 * rows), 2, rows, tb)
        )
        return 0

    lax.fori_loop(0, ncol, silu_body, 0)

    h_send(0, 1, (2, 3))
    h_send(0, 1, (0, 1))
    send_own(0, 1)
    relay(0, 0)
    send_own(0, 2)
    h_relay(0, 1)
    relay(0, 1)
    send_own(1, 1)
    h_send(1, 4, (2, 3))
    relay(0, 2)
    give_opp(0, 0)
    h_send(4, 5, (2, 3))
    h_send(1, 2, (0, 1))
    h_wait(0, 1)
    pair(0, 0, 4)
    h_send(2, 3, (0, 1))
    give_opp(0, 1)
    h_relay(1, 4)
    pair(0, 1, 4)
    h_send(3, 4, (0, 1))
    give_opp(0, 2)
    h_relay(4, 5)
    relay(1, 1)
    h_send(4, 5, (0, 1))
    pair(0, 2, 4)
    send_own(1, 2)
    h_send(5, 7, (2, 3))
    h_send(5, 6, (0, 1))
    h_wait(1, 3)
    pair(0, 0, 3)
    h_send(6, 7, (0, 1))
    pair(0, 1, 3)
    send_own(1, 0)
    relay(1, 2)
    pair(0, 2, 3)
    h_relay(5, 7)
    give_opp(1, 1)
    h_send(7, 8, (2, 3))
    h_wait(3, 5)
    pair(0, 0, 2)
    h_send(7, 8, (0, 1))
    pre(1, 1, 4, 3, 2)
    give_opp(1, 2)
    pair(0, 1, 2)
    relay(1, 0)
    pair(1, 2, 4)
    pair(0, 2, 2)
    h_relay(7, 8)
    h_wait(5, 7)
    pair(0, 0, 1)
    pre(1, 1, 1)
    pair(1, 1, 4)
    give_opp(1, 0)
    pair(0, 1, 1)
    h_wait(7, 8)
    pre(1, 0, 4, 3, 2, 1, 0)
    pre(1, 1, 0)
    pair(1, 2, 3)
    pair(1, 1, 3)
    pair(0, 2, 1)
    pair(0, 0, 0)
    pair(1, 0, 4)
    pair(0, 1, 0)
    pair(1, 2, 2)
    pair(1, 1, 2)
    pair(1, 0, 3)
    pair(0, 2, 0)
    pair(1, 2, 1)
    pair(1, 0, 2)
    pair(1, 1, 1)
    pair(1, 0, 1)
    pair(1, 2, 0)
    pair(1, 1, 0)
    pair(1, 0, 0)
    finish(0)
    finish(1)

    n_x, n_c, n_p = 2 * nu - len(ACROSS), 1 + len(ACROSS), len(Y_FIRST)
    wait_out(gbuf.at[pl.ds(0, n_x), pl.ds(0, 3)], to_x)
    wait_out(gbuf.at[pl.ds(0, 2 * nu)], to_partner)
    wait_out(gbuf.at[pl.ds(0, n_c), pl.ds(0, 3)], to_cross)
    wait_out(ht, of_h)
    wait_out(zs.at[:, pl.ds(0, 2 * nu - n_p), pl.ds(0, 2 * far - 1)], zsend_sem.at[0])
    wait_out(zs.at[0, pl.ds(0, n_p), pl.ds(0, 2 * far - 1)], zsend_sem.at[1])
    wait_out(ys.at[pl.ds(0, 4 * nu - 2 * n_p)], to_y)
    wait_out(yps.at[:, pl.ds(0, far)], to_yp)


def run(gate_pre, up_pre, out_grad, w=256, nz=NZ, interpret=False):
    tb, hidden = gate_pre.shape
    rows = hidden // (NX * nz * 2)
    nu = out_grad.shape[1] // w
    features = 4 * out_grad.shape[1]
    far = nz // 2
    bf16 = jnp.bfloat16
    wide = 2 * rows * nz // 2
    ncol = hidden // wide
    n = 4 * nu
    dma = pltpu.SemaphoreType.DMA
    return pl.pallas_call(
        functools.partial(kernel, (tb, rows, w, nu, nz)),
        out_shape=jax.ShapeDtypeStruct((rows, features), bf16),
        in_specs=[pl.BlockSpec(memory_space=pl.ANY)] * 3,
        out_specs=pl.BlockSpec(memory_space=pltpu.VMEM),
        scratch_shapes=[
            pltpu.VMEM((ncol, 2, tb, wide), bf16),
            pltpu.VMEM((NX, nz, 2, rows, tb), bf16),
            pltpu.VMEM((3, nz, 2, rows, tb), bf16),
            pltpu.VMEM((2, nz, rows, tb), bf16),
            pltpu.VMEM((n, 4, tb, w), bf16),
            pltpu.VMEM((2, far, n, 2, rows, w), bf16),
            pltpu.VMEM((2, far, n, 2, rows, w), bf16),
            pltpu.VMEM((n, 2, rows, w), jnp.float32),
            pltpu.VMEM((n, rows, w), bf16),
            pltpu.VMEM((n, rows, w), bf16),
            pltpu.VMEM((2 * len(Y_FIRST), far + 1, 2, rows, w), bf16),
            pltpu.VMEM((2 * len(Y_FIRST), far + 1, 2, rows, w), bf16),
            dma((ncol,)),
            dma((nu,)),
            dma((6,)),
            dma((2,)),
            dma((2 * nu,)),
            dma((2 * nu,)),
            dma((2 * nu,)),
            dma((nu,)),
            dma((2, nu)),
            dma((nz,)),
            dma((nz,)),
            dma((far, n)),
            dma((2 * nu,)),
            dma((2 * len(Y_FIRST), far + 1)),
        ],
        compiler_params=pltpu.CompilerParams(
            collective_id=0, has_side_effects=True, vmem_limit_bytes=60 * 1024 * 1024
        ),
        interpret=interpret,
    )(gate_pre, up_pre, out_grad)


def solution(mesh):
    return jax.shard_map(
        run,
        mesh=mesh,
        in_specs=(P("dp", "mp"), P("dp", "mp"), P("dp", "mp")),
        out_specs=P(("mp", "dp"), None),
        check_vma=False,
    )
```
